32 devices in a mesh: dom: 8 (over z, x), group: 4 (over y, core).
Axes of the slice: x: 2, y: 2, z: 4, core: 2. Of those that a mesh axis runs over, the one named last changes fastest.
Arguments:
- features: bfloat16 [65536, 256], P(('dom', 'group')), may hold values from -6 to 6
- boundary: int32 [2048], P(('dom', 'group')), may hold values from 0 to 127, as said below
- request: int32 [128, 24], P(('dom', 'group')), may hold values from 0 to 63, as said below
- tile_slots: int32 [512, 8], P(('dom', 'group')), may hold values from 0 to 223, as said below
- neighbors: int32 [65536, 10], P(('dom', 'group')), may hold values from 0 to 127
- negatives: int32 [65536, 4], P(('dom', 'group')), may hold values from 0 to 127
- layer_weight: bfloat16 [512, 256], replicated, may hold values from -0.25 to 0.25
Outputs:
- feature_grad: float32 [65536, 256], P(('dom', 'group'))
- weight_grad: float32 [512, 256], replicated
- loss_mean: float32 [], replicated
The draws below stay inside these ranges and needn't reach their ends.
Inputs may be any that keep to these rules, and one draw needn't show every extreme that they name: The 64 entries boundary[i * 64 to i * 64 + 63] are distinct numbers of device i's own row blocks. `request`: row i * 4 + e holds 24 distinct positions in the boundary list of device (i // 4) * 4 + e. `tile_slots`: entries are numbers s as in the first step; the 128 entries of one device are distinct and include every number from 128 to 223.
All inputs are finite; a program needn't handle non-finite values.
Results may differ from the reference program's by a relative error of at most 0.00075.
The reference program's roundings to bfloat16 on the way (of `candidates`, `counts`, `aggregate`, `embed_half`, `dscores`, `dpreact` and `daggregate`) count: a program that leaves them out, or rounds other values in their place, can miss the bound.
Values may be sent and summed in bfloat16 or wider, within the bound.
No kernel may reach another device: no remote copies, remote signals or barrier semaphores. Data moves between devices by JAX's collectives and lax.ppermute only.
A program may use at most 64 MiB of HBM per device.

```python
import jax
import jax.numpy as jnp
from jax import lax

D = 256
NODE_DEV = 2048
TILE = 128
BLK = 16
NBT = 8
DEG = 10
NNEG = 4
TILES = 16
NBD = 128
CAND = 128
PEERS = 4
DEVS = 32
NODES = 65536
CAP = 24
NBND = 64


def draw_boundary(key, part):
    row_keys = jax.random.split(jax.random.fold_in(key, 3), DEVS)
    picked = jax.vmap(lambda single: jax.random.permutation(single, NBD)[:NBND])(row_keys)
    return picked.reshape(-1).astype(jnp.int32)


def draw_request(key, part):
    row_keys = jax.random.split(jax.random.fold_in(key, 5), DEVS * PEERS)
    picked = jax.vmap(lambda single: jax.random.permutation(single, NBND)[:CAP])(row_keys)
    return picked.astype(jnp.int32)


def draw_tile_slots(key, part):
    folded = jax.random.fold_in(key, 7)
    key_noise, key_mix = jax.random.split(folded, 2)
    received_count = PEERS * CAP
    slot_total = NBD + received_count
    priority = jnp.concatenate([jnp.ones((DEVS, NBD), jnp.int32), 2 * jnp.ones((DEVS, received_count), jnp.int32)], axis=1)
    jitter = jax.random.randint(key_noise, (DEVS, slot_total), 0, 1024, dtype=jnp.int32)
    scored = priority * 4194304 + jitter * slot_total + jnp.arange(slot_total, dtype=jnp.int32)[None, :]
    chosen = lax.top_k(scored, TILES * NBT)[1].astype(jnp.int32)
    shuffle = jax.random.split(key_mix, DEVS)
    mixed = jax.vmap(lambda single, chosen_row: jax.random.permutation(single, chosen_row))(shuffle, chosen)
    return mixed.reshape(DEVS * TILES, NBT).astype(jnp.int32)


def plant(result, rng, smallest, top_value):
    longest = result.shape.index(max(result.shape))
    spots = []
    for shift in (0, 1):
        where = [jax.random.randint(jax.random.fold_in(rng, axis), (), 0, length) for axis, length in enumerate(result.shape)]
        where[longest] = (where[longest] + shift) % result.shape[longest]
        spots.append(tuple(where))
    return result.at[spots[0]].set(smallest).at[spots[1]].set(top_value)


def levels(stream_key, extent, shards, smallest, largest):
    def one(dim, blocks):
        heights = jax.random.uniform(jax.random.fold_in(jax.random.fold_in(stream_key, 6), dim), (blocks,), jnp.float32, smallest / len(shards), largest / len(shards))
        return jnp.repeat(jnp.exp(heights), extent[dim] // blocks).reshape((-1,) + (1,) * (len(extent) - dim - 1))

    loudness = one(*shards[0])
    for cut in shards[1:]:
        loudness = loudness * one(*cut)
    return loudness


def gaussian(stream_key, extent, scale, reach, cuts=(), held_as=jnp.bfloat16):
    factor_of = levels(stream_key, extent, cuts, -0.22, 0.18) if cuts else 1.0
    entries = jax.random.normal(stream_key, extent, jnp.float32) * scale * factor_of
    return jnp.minimum(jnp.maximum(entries, -reach), reach).astype(held_as)


def setup_inputs(seed: int = 0) -> dict:
    streams_of = jax.random.split(jax.random.key(seed), 8)
    features = gaussian(streams_of[0], (NODES, D), 1.0, 6.0, ((0, 32),))
    boundary = draw_boundary(jax.random.fold_in(streams_of[7], 71), 0)
    request = draw_request(jax.random.fold_in(streams_of[7], 71), 0)
    tile_slots = draw_tile_slots(jax.random.fold_in(streams_of[7], 71), 0)
    neighbors = plant(jax.random.randint(streams_of[4], (NODES, DEG), 0, CAND), jax.random.fold_in(streams_of[4], 1), 0, CAND - 1).astype(jnp.int32)
    negatives = plant(jax.random.randint(streams_of[5], (NODES, NNEG), 0, CAND), jax.random.fold_in(streams_of[5], 1), 0, CAND - 1).astype(jnp.int32)
    layer_weight = gaussian(streams_of[6], (2 * D, D), (2 * D) ** -0.5, 0.25)
    return {"features": features, "boundary": boundary, "request": request, "tile_slots": tile_slots, "neighbors": neighbors, "negatives": negatives, "layer_weight": layer_weight}


margin = 0.5
epsilon = 1e-06

def contract(form, left, right):
    return jnp.einsum(form, left.astype(jnp.float32), right.astype(jnp.float32))

def tile_terms(own_rows, candidates, neighbor_ids, negative_ids, layer_weight):
    tile_count, tile_rows, feature_width = own_rows.shape
    cand_count = candidates.shape[1]
    degree = neighbor_ids.shape[-1]
    negative_count = negative_ids.shape[-1]
    slot_ids = jnp.arange(cand_count, dtype=jnp.int32)
    counts = lax.optimization_barrier(jnp.sum((neighbor_ids[..., None] == slot_ids).astype(jnp.float32), axis=2)).astype(jnp.bfloat16)
    aggregate = (contract('tuc,tcd->tud', counts, candidates) / degree).astype(jnp.bfloat16)
    joined = jnp.concatenate([own_rows, aggregate], axis=-1).reshape(-1, 2 * feature_width)
    preact = jnp.dot(joined, layer_weight, preferred_element_type=jnp.float32)
    gate_value = jax.nn.sigmoid(preact)
    hidden = preact * gate_value
    norm_scale = lax.rsqrt(lax.optimization_barrier(jnp.mean(hidden * hidden, axis=-1, keepdims=True)) + epsilon)
    embedding = hidden * norm_scale
    embed_half = embedding.astype(jnp.bfloat16).reshape(tile_count, tile_rows, feature_width)
    inv_root = feature_width ** (-0.5)
    scores = contract('tud,tcd->tuc', embed_half, candidates) * inv_root
    positive = (neighbor_ids[..., 0:1] == slot_ids).astype(jnp.float32)
    negative = (negative_ids[..., None] == slot_ids).astype(jnp.float32)
    pos_score = lax.optimization_barrier(jnp.sum(scores * positive, axis=-1, keepdims=True))
    neg_score = lax.optimization_barrier(jnp.sum(scores[:, :, None, :] * negative, axis=-1))
    excess = margin + neg_score - pos_score
    loss_sum = jnp.sum(jax.nn.softplus(excess)) / negative_count
    neg_weight = jax.nn.sigmoid(excess) / negative_count
    dscores = (lax.optimization_barrier(jnp.sum(neg_weight[..., None] * negative, axis=2)) - lax.optimization_barrier(jnp.sum(neg_weight, axis=-1, keepdims=True)) * positive) * inv_root
    dscores_half = dscores.astype(jnp.bfloat16)
    dembedding = contract('tuc,tcd->tud', dscores_half, candidates).reshape(-1, feature_width)
    dcandidates = contract('tuc,tud->tcd', dscores_half, embed_half)
    dhidden = norm_scale * (dembedding - embedding * lax.optimization_barrier(jnp.mean(dembedding * embedding, axis=-1, keepdims=True)))
    dpreact = (dhidden * gate_value * (1.0 + preact * (1.0 - gate_value))).astype(jnp.bfloat16)
    dweight = jnp.dot(joined.T, dpreact, preferred_element_type=jnp.float32)
    dinputs = jnp.dot(dpreact, layer_weight.T, preferred_element_type=jnp.float32)
    dself = dinputs[:, :feature_width].reshape(tile_count, tile_rows, feature_width)
    daggregate = (dinputs[:, feature_width:] / degree).astype(jnp.bfloat16).reshape(tile_count, tile_rows, feature_width)
    dcandidates = dcandidates + contract('tuc,tud->tcd', counts, daggregate)
    return (loss_sum, dweight, dself, dcandidates)

def reference(features, boundary, request, tile_slots, neighbors, negatives, layer_weight):
    all_blocks = features.reshape(-1, BLK, D)

    def device_step(carried, device):
        gradients, dweight_sum, loss_total = carried
        slot_list = lax.dynamic_slice_in_dim(tile_slots, device * TILES, TILES).reshape(-1)
        wanted = lax.dynamic_slice_in_dim(request, device * PEERS, PEERS).reshape(-1)
        received_slot = jnp.clip(slot_list - NBD, 0, PEERS * CAP - 1)
        peer_index = received_slot // CAP
        owner_device = device // PEERS * PEERS + peer_index
        position = wanted[received_slot]
        local_block = boundary[owner_device * NBND + position]
        remote = owner_device * NBD + local_block
        block_ids = jnp.where(slot_list < NBD, device * NBD + slot_list, remote).astype(jnp.int32)
        candidates = all_blocks[block_ids].reshape(TILES, CAND, D)
        own_rows = lax.dynamic_slice_in_dim(features, device * NODE_DEV, NODE_DEV).reshape(TILES, TILE, D)
        neighbor_ids = lax.dynamic_slice_in_dim(neighbors, device * NODE_DEV, NODE_DEV).reshape(TILES, TILE, DEG)
        negative_ids = lax.dynamic_slice_in_dim(negatives, device * NODE_DEV, NODE_DEV).reshape(TILES, TILE, NNEG)
        loss_sum, dweight, dself, dcandidates = tile_terms(own_rows, candidates, neighbor_ids, negative_ids, layer_weight)
        current = lax.dynamic_slice_in_dim(gradients, device * NBD, NBD)
        gradients = lax.dynamic_update_slice_in_dim(gradients, current + dself.reshape(NBD, BLK, D), device * NBD, 0)
        gradients = gradients.at[block_ids].add(dcandidates.reshape(-1, BLK, D))
        return ((gradients, dweight_sum + dweight, loss_total + loss_sum), None)
    start = (jnp.zeros((DEVS * NBD, BLK, D), jnp.float32), jnp.zeros((2 * D, D), jnp.float32), jnp.zeros((), jnp.float32))
    finished, _ = lax.scan(device_step, start, jnp.arange(DEVS, dtype=jnp.int32))
    gradients, dweight_sum, loss_total = finished
    return (gradients.reshape(-1, D), dweight_sum / NODE_DEV, loss_total / NODES)
```

```python
import functools

import jax
import jax.numpy as jnp
from jax import lax
from jax.experimental import pallas as pl
from jax.experimental.pallas import tpu as pltpu
from jax.sharding import PartitionSpec as P

TILE = 128
BLK = 16
NBT = 8
PAD = 8
CHUNK = 4

margin = 0.5
epsilon = 1e-06

VMEM = pl.BlockSpec(memory_space=pltpu.VMEM)
SMEM = pl.BlockSpec(memory_space=pltpu.SMEM)
f32 = jnp.float32
bf16 = jnp.bfloat16


def dot(left, right, dims):
    return lax.dot_general(left, right, (dims, ((), ())), preferred_element_type=f32)


def call(kernel, out_shape, args, specs, out_specs, scratch=(), flops=0, name=None):
    size = sum(a.size * a.dtype.itemsize for a in args)
    return pl.pallas_call(
        kernel,
        out_shape=out_shape,
        in_specs=specs,
        out_specs=out_specs,
        scratch_shapes=list(scratch),
        cost_estimate=pl.CostEstimate(flops=flops, bytes_accessed=size, transcendentals=0),
        name=name,
    )(*args)


def share_kernel(boundary, request, feat, out):
    count = boundary.shape[0]

    def body(i, carry):
        out[i] = feat[boundary[i]]
        return carry

    lax.fori_loop(0, count, body, 0, unroll=8)
    rows, cols = request.shape
    row_ids = lax.broadcasted_iota(jnp.int32, (BLK, 128), 0)
    lane_ids = lax.broadcasted_iota(jnp.int32, (BLK, 128), 1)
    tag = jnp.zeros((BLK, 128), f32)
    for r in range(rows):
        for c in range(cols):
            tag = jnp.where((row_ids == r) & (lane_ids == c), request[r, c].astype(f32), tag)
    out[count] = jnp.zeros((BLK, feat.shape[2]), bf16)
    out[count, :, 0:128] = tag.astype(bf16)


def early_kernel(feat, weight, nbr, counts, pre):
    rows, width = feat.shape
    degree = nbr.shape[0]
    cand_ids = lax.broadcasted_iota(jnp.int32, (TILE, TILE), 0)
    top = weight[0:width, :]

    def body(t, carry):
        at = pl.ds(pl.multiple_of(t * TILE, TILE), TILE)
        ids = nbr[:, at]
        total = jnp.zeros((TILE, TILE), f32)
        for j in range(degree):
            total = total + jnp.where(ids[j : j + 1, :] == cand_ids, 1.0, 0.0)
        counts[at, :] = total.astype(bf16)
        return carry

    lax.fori_loop(0, rows // TILE, body, 0)
    step = CHUNK * TILE

    def dense(c, carry):
        at = pl.ds(pl.multiple_of(c * step, step), step)
        pre[at, :] = dot(feat[at, :], top, ((1,), (0,)))
        return carry

    lax.fori_loop(0, rows // step, dense, 0)


def main_kernel(peers, slots, request, boundary, feat3, feat, weight, nbr, neg, pre, counts, *rest):
    pieces = rest[: peers - 1]
    own, keep, send = rest[peers - 1 : peers + 2]
    back = rest[peers + 2 : 2 * peers + 1]
    cand, agg, dpre, dcand, where_own, where_slot, wgrad, losses = rest[2 * peers + 1 :]
    rows, width = feat.shape
    blocks = feat3.shape[0]
    capacity = request.shape[1]
    degree = nbr.shape[0]
    negs = neg.shape[0]
    me = lax.axis_index("group")

    def gather(i, carry):
        t = i // NBT
        s = slots[i - t * NBT, t]
        local = s < blocks
        r = jnp.maximum(s - blocks, 0)
        e = r // capacity
        at = request[e, r - e * capacity]
        k = e ^ me
        mine = local | (k == 0)
        own_at = jnp.where(local, jnp.minimum(s, blocks - 1), boundary[at])
        where_own[i] = jnp.where(mine, own_at, -1)

        @pl.when(jnp.logical_not(local))
        def _():
            where_slot[r] = i

        value = feat3[own_at]
        for p in range(1, peers):
            value = jnp.where(jnp.logical_not(mine) & (k == p), pieces[p - 1][at], value)
        cand[i] = value
        return carry

    lax.fori_loop(0, blocks, gather, 0)
    losses[...] = jnp.zeros(losses.shape, f32)
    top = weight[0:width, :]
    low = weight[width : 2 * width, :]
    cand_ids = lax.broadcasted_iota(jnp.int32, (TILE, TILE), 0)
    step = CHUNK * TILE
    inv_root = width ** (-0.5)

    def chunk(c, carry):
        at = pl.ds(pl.multiple_of(c * step, step), step)
        tiles = []
        for tt in range(CHUNK):
            t = c * CHUNK + tt
            cd = cand[pl.ds(t * NBT, NBT)].reshape(TILE, width)
            ct = counts[pl.ds(pl.multiple_of(t * TILE, TILE), TILE), :]
            tiles.append((cd, ct))
            part = (dot(ct, cd, ((0,), (0,))) / degree).astype(bf16)
            agg[pl.ds(pl.multiple_of(t * TILE, TILE), TILE), :] = part
        preact = pre[at, :] + dot(agg[at, :], low, ((1,), (0,)))
        gate = jax.nn.sigmoid(preact)
        hidden = preact * gate
        scale = lax.rsqrt(jnp.mean(hidden * hidden, axis=-1, keepdims=True) + epsilon)
        embedding = hidden * scale
        half = embedding.astype(bf16)
        demb = []
        dsc = []
        for tt in range(CHUNK):
            t = c * CHUNK + tt
            lanes = pl.ds(pl.multiple_of(t * TILE, TILE), TILE)
            cd, ct = tiles[tt]
            scores = dot(cd, half[tt * TILE : (tt + 1) * TILE, :], ((1,), (1,))) * inv_root
            first = nbr[:, lanes][0:1, :] == cand_ids
            ids = neg[:, lanes]
            hits = [ids[n : n + 1, :] == cand_ids for n in range(negs)]
            pos = jnp.sum(jnp.where(first, scores, 0.0), axis=0, keepdims=True)
            picked = jnp.concatenate(
                [jnp.sum(jnp.where(h, scores, 0.0), axis=0, keepdims=True) for h in hits], axis=0
            )
            excess = margin + picked - pos
            soft = jnp.maximum(excess, 0.0) + jnp.log1p(jnp.exp(-jnp.abs(excess)))
            losses[0:negs, :] += soft
            weights = jax.nn.sigmoid(excess) / negs
            total = jnp.sum(weights, axis=0, keepdims=True)
            ds = jnp.zeros((TILE, TILE), f32)
            for n in range(negs):
                ds = ds + jnp.where(hits[n], weights[n : n + 1, :], 0.0)
            ds = ((ds - jnp.where(first, total, 0.0)) * inv_root).astype(bf16)
            dsc.append(ds)
            demb.append(dot(ds, cd, ((0,), (0,))))
        demb = jnp.concatenate(demb, axis=0)
        mean = jnp.mean(demb * embedding, axis=-1, keepdims=True)
        dhidden = scale * (demb - embedding * mean)
        dp = (dhidden * gate * (1.0 + preact * (1.0 - gate))).astype(bf16)
        dpre[at, :] = dp
        own[pl.ds(c * (step // BLK), step // BLK)] = dot(dp, top, ((1,), (1,))).reshape(
            step // BLK, BLK, width
        )
        dagg = (dot(dp, low, ((1,), (1,))) / degree).astype(bf16)
        for tt in range(CHUNK):
            t = c * CHUNK + tt
            cd, ct = tiles[tt]
            part = slice(tt * TILE, (tt + 1) * TILE)
            got = dot(dsc[tt], half[part, :], ((1,), (0,))) + dot(ct, dagg[part, :], ((1,), (0,)))
            dcand[pl.ds(t * NBT, NBT)] = got.reshape(NBT, BLK, width)
        return carry

    lax.fori_loop(0, rows // step, chunk, 0)

    wgrad[0:width, :] = dot(feat[...], dpre[...], ((0,), (0,)))
    wgrad[width : 2 * width, :] = dot(agg[...], dpre[...], ((0,), (0,)))
    half_rows = width
    core = me & 1
    keep[0:half_rows, :] = wgrad[pl.ds(pl.multiple_of(core * half_rows, half_rows), half_rows), :]
    send[0:half_rows, :] = wgrad[
        pl.ds(pl.multiple_of((1 - core) * half_rows, half_rows), half_rows), :
    ]
    loss = jnp.sum(losses[...]) / negs
    spread = jnp.full((PAD, width), loss, f32)
    keep[half_rows : half_rows + PAD, :] = spread
    send[half_rows : half_rows + PAD, :] = spread

    def scatter(i, carry):
        d = where_own[i]
        to = jnp.maximum(d, 0)
        own[to] = own[to] + jnp.where(d >= 0, dcand[i], 0.0)
        return carry

    lax.fori_loop(0, blocks, scatter, 0, unroll=4)
    for k in range(1, peers):
        base = (me ^ k) * capacity

        def outgo(c, carry, k=k, base=base):
            back[k - 1][c] = dcand[where_slot[base + c]]
            return carry

        lax.fori_loop(0, capacity, outgo, 0, unroll=4)


def return_kernel(boundary, asked, own_in, *rest):
    grads, own = rest[:-1], rest[-1]
    own[...] = own_in[...]
    capacity = asked.shape[1]
    for k, got in enumerate(grads):

        def body(c, carry, k=k, got=got):
            to = boundary[asked[k, c]]
            own[to] = own[to] + got[c]
            return carry

        lax.fori_loop(0, capacity, body, 0, unroll=4)


def finish_kernel(rows, nodes, mine, other, wgrad, loss):
    half_rows = mine.shape[0] - PAD
    core = lax.axis_index("group") & 1
    wgrad[pl.ds(pl.multiple_of(core * half_rows, half_rows), half_rows), :] = (
        mine[0:half_rows, :] / rows
    )
    wgrad[pl.ds(pl.multiple_of((1 - core) * half_rows, half_rows), half_rows), :] = (
        other[0:half_rows, :] / rows
    )
    first = jnp.where(core == 0, mine[half_rows:, 0:128], other[half_rows:, 0:128])
    loss[0, 0] = jnp.max(first) / nodes


def per_device(features, boundary, request, tile_slots, neighbors, negatives, layer_weight):
    row_count, width = features.shape
    peers = lax.axis_size("group")
    domains = lax.axis_size("dom")
    devices = peers * domains
    capacity = request.shape[1]
    bound_count = boundary.shape[0]
    block_count = row_count // BLK
    blocks = features.reshape(block_count, BLK, width)
    nbr = neighbors.T
    neg = negatives.T
    slots = tile_slots.T
    sds = jax.ShapeDtypeStruct

    shared = call(
        share_kernel,
        sds((bound_count + 1, BLK, width), bf16),
        (boundary, request, blocks),
        [SMEM, SMEM, VMEM],
        VMEM,
        name="share",
    )
    pieces = {0: shared}
    bit = peers // 2
    while bit:
        for k in list(pieces):
            pairs = [(i, i ^ bit) for i in range(peers)]
            pieces[k | bit] = lax.ppermute(pieces[k], "group", pairs)
        bit //= 2

    counts, pre = call(
        early_kernel,
        (sds((row_count, TILE), bf16), sds((row_count, width), f32)),
        (features, layer_weight, nbr),
        [VMEM] * 3,
        (VMEM, VMEM),
        flops=2 * row_count * width * width * 8,
        name="early",
    )
    outs = call(
        functools.partial(main_kernel, peers),
        (
            sds((block_count, BLK, width), f32),
            sds((width + PAD, width), f32),
            sds((width + PAD, width), f32),
        )
        + (sds((capacity, BLK, width), f32),) * (peers - 1),
        (slots, request, boundary, blocks, features, layer_weight, nbr, neg, pre, counts)
        + tuple(pieces[k] for k in range(1, peers)),
        [SMEM] * 3 + [VMEM] * (6 + peers),
        (VMEM,) * (peers + 2),
        scratch=(
            pltpu.VMEM((block_count, BLK, width), bf16),
            pltpu.VMEM((row_count, width), bf16),
            pltpu.VMEM((row_count, width), bf16),
            pltpu.VMEM((block_count, BLK, width), f32),
            pltpu.SMEM((block_count,), jnp.int32),
            pltpu.SMEM((peers * capacity,), jnp.int32),
            pltpu.VMEM((2 * width, width), f32),
            pltpu.VMEM((8, TILE), f32),
        ),
        flops=2 * row_count * width * width * 20,
        name="main",
    )
    own, keep, send = outs[:3]
    back = outs[3:]

    everyone = ("dom", "group")

    def swap(x, masks):
        return lax.ppermute(x, everyone, [(i, i ^ masks[i & 1]) for i in range(devices)])

    grads = [
        lax.ppermute(back[k - 1], "group", [(i, i ^ k) for i in range(peers)])
        for k in range(1, peers)
    ]
    total = keep + swap(send, (1, 1))
    bits = devices.bit_length() - 1
    masks = [1 << b for b in range(1, bits)][::-1]
    masks = [masks[1], masks[0] | masks[1]] + masks[2:]
    for s in range(len(masks)):
        other = s ^ 1 if (s ^ 1) < len(masks) else s
        total = total + swap(total, (masks[s], masks[other]))
    partner = swap(total, (1, 1))
    weight_grad, loss = call(
        functools.partial(finish_kernel, row_count, row_count * devices),
        (sds((2 * width, width), f32), sds((1, 1), f32)),
        (total, partner),
        [VMEM, VMEM],
        (VMEM, SMEM),
        name="finish",
    )

    me = lax.axis_index("group")
    asked = jnp.stack(
        [
            lax.dynamic_slice_in_dim(pieces[k][bound_count], me, 1)[0, :capacity]
            for k in range(1, peers)
        ]
    ).astype(jnp.int32)
    feature_grad = call(
        return_kernel,
        sds((block_count, BLK, width), f32),
        (boundary, asked, own) + tuple(grads),
        [SMEM, SMEM] + [VMEM] * peers,
        VMEM,
        name="return",
    )
    return feature_grad.reshape(row_count, width), weight_grad, loss.reshape(())


def solution(mesh):
    return jax.shard_map(
        per_device,
        mesh=mesh,
        in_specs=(
            P(("dom", "group"), None),
            P(("dom", "group")),
            P(("dom", "group"), None),
            P(("dom", "group"), None),
            P(("dom", "group"), None),
            P(("dom", "group"), None),
            P(),
        ),
        out_specs=(P(("dom", "group"), None), P(), P()),
        check_vma=False,
    )
```

```python
import functools

import jax
import jax.numpy as jnp
from jax import lax
from jax.experimental import pallas as pl
from jax.experimental.pallas import tpu as pltpu
from jax.sharding import PartitionSpec as P


TILE = 128
BLK = 16
NBT = 8
PAD = 8
CHUNK = 4


margin = 0.5
epsilon = 1e-06

VMEM = pl.BlockSpec(memory_space=pltpu.VMEM)
SMEM = pl.BlockSpec(memory_space=pltpu.SMEM)
f32 = jnp.float32
bf16 = jnp.bfloat16


def dot(left, right, dims):
    return lax.dot_general(left, right, (dims, ((), ())), preferred_element_type=f32)


def call(kernel, out_shape, args, specs, out_specs, scratch=(), flops=0, limit=8):
    size = sum(a.size * a.dtype.itemsize for a in args)
    return pl.pallas_call(
        kernel,
        out_shape=out_shape,
        in_specs=specs,
        out_specs=out_specs,
        scratch_shapes=list(scratch),
        cost_estimate=pl.CostEstimate(flops=flops, bytes_accessed=size, transcendentals=0),
        compiler_params=pltpu.CompilerParams(vmem_limit_bytes=limit << 20),
    )(*args)


def share_kernel(boundary, request, feat, out):
    count = boundary.shape[0]

    def body(i, carry):
        out[i] = feat[boundary[i]]
        return carry

    lax.fori_loop(0, count, body, 0, unroll=8)
    rows, cols = request.shape
    row_ids = lax.broadcasted_iota(jnp.int32, (BLK, 128), 0)
    lane_ids = lax.broadcasted_iota(jnp.int32, (BLK, 128), 1)
    tag = jnp.zeros((BLK, 128), f32)
    for r in range(rows):
        for c in range(cols):
            tag = jnp.where((row_ids == r) & (lane_ids == c), request[r, c].astype(f32), tag)
    out[count] = jnp.zeros((BLK, feat.shape[2]), bf16)
    out[count, :, 0:128] = tag.astype(bf16)


def early_kernel(slots, request, boundary, feat, weight, nbr, counts, pre, where_own, where_slot):
    rows, width = feat.shape
    blocks = where_own.shape[0]
    capacity = request.shape[1]
    me = lax.axis_index("group")

    def place(i, carry):
        t = i // NBT
        s = slots[i - t * NBT, t]
        local = s < blocks
        r = jnp.maximum(s - blocks, 0)
        e = r // capacity
        at = request[e, r - e * capacity]
        mine = local | (e == me)
        own_at = jnp.where(local, s, boundary[at])
        where_own[i] = jnp.where(mine, own_at, -1)
        spare = where_slot.shape[0] - 1
        where_slot[jnp.where(local, spare, r)] = i
        return carry

    lax.fori_loop(0, blocks, place, 0, unroll=4)
    degree = nbr.shape[0]
    cand_ids = lax.broadcasted_iota(jnp.int32, (TILE, TILE), 0)
    top = weight[0:width, :]

    def body(t, carry):
        at = pl.ds(pl.multiple_of(t * TILE, TILE), TILE)
        ids = nbr[:, at]
        total = jnp.zeros((TILE, TILE), f32)
        for j in range(degree):
            total = total + jnp.where(ids[j : j + 1, :] == cand_ids, 1.0, 0.0)
        counts[at, :] = total.astype(bf16)
        return carry

    lax.fori_loop(0, rows // TILE, body, 0)
    step = CHUNK * TILE

    def dense(c, carry):
        at = pl.ds(pl.multiple_of(c * step, step), step)
        pre[at, :] = dot(feat[at, :], top, ((1,), (0,)))
        return carry

    lax.fori_loop(0, rows // step, dense, 0)


def main_kernel(peers, request, where_own, where_slot, feat, weight, nbr, neg, pre, counts, *rest):
    pieces = rest[: peers - 1]
    own, keep, send = rest[peers - 1 : peers + 2]
    back = rest[peers + 2 : 2 * peers + 1]
    cand, agg, dpre, dcand, wgrad, losses = rest[2 * peers + 1 :]
    blocks, _, width = feat.shape
    rows = blocks * BLK
    capacity = request.shape[1]
    degree = nbr.shape[0]
    negs = neg.shape[0]
    me = lax.axis_index("group")

    def fetch(i, carry):
        cand[i] = feat[jnp.maximum(where_own[i], 0)]
        return carry

    lax.fori_loop(0, blocks, fetch, 0, unroll=8)
    for k in range(1, peers):
        peer = me ^ k

        def fetch_far(c, carry, k=k, peer=peer):
            cand[where_slot[peer * capacity + c]] = pieces[k - 1][request[peer, c]]
            return carry

        lax.fori_loop(0, capacity, fetch_far, 0, unroll=8)
    losses[...] = jnp.zeros(losses.shape, f32)
    top = weight[0:width, :]
    low = weight[width : 2 * width, :]
    cand_ids = lax.broadcasted_iota(jnp.int32, (TILE, TILE), 0)
    step = CHUNK * TILE
    inv_root = width ** (-0.5)

    def chunk(c, carry):
        at = pl.ds(pl.multiple_of(c * step, step), step)
        tiles = []
        for tt in range(CHUNK):
            t = c * CHUNK + tt
            cd = cand[pl.ds(t * NBT, NBT)].reshape(TILE, width)
            ct = counts[pl.ds(pl.multiple_of(t * TILE, TILE), TILE), :]
            tiles.append((cd, ct))
            part = (dot(ct, cd, ((0,), (0,))) / degree).astype(bf16)
            agg[pl.ds(pl.multiple_of(t * TILE, TILE), TILE), :] = part
        preact = pre[at, :] + dot(agg[at, :], low, ((1,), (0,)))
        gate = jax.nn.sigmoid(preact)
        hidden = preact * gate
        scale = lax.rsqrt(jnp.mean(hidden * hidden, axis=-1, keepdims=True) + epsilon)
        embedding = hidden * scale
        half = embedding.astype(bf16)
        demb = []
        dsc = []
        for tt in range(CHUNK):
            t = c * CHUNK + tt
            lanes = pl.ds(pl.multiple_of(t * TILE, TILE), TILE)
            cd, ct = tiles[tt]
            scores = dot(cd, half[tt * TILE : (tt + 1) * TILE, :], ((1,), (1,))) * inv_root
            first = nbr[:, lanes][0:1, :] == cand_ids
            ids = neg[:, lanes]
            hits = [ids[n : n + 1, :] == cand_ids for n in range(negs)]
            pos = jnp.sum(jnp.where(first, scores, 0.0), axis=0, keepdims=True)
            picked = jnp.concatenate(
                [jnp.sum(jnp.where(h, scores, 0.0), axis=0, keepdims=True) for h in hits], axis=0
            )
            excess = margin + picked - pos
            soft = jnp.maximum(excess, 0.0) + jnp.log1p(jnp.exp(-jnp.abs(excess)))
            losses[0:negs, :] += soft
            weights = jax.nn.sigmoid(excess) / negs
            total = jnp.sum(weights, axis=0, keepdims=True)
            ds = jnp.zeros((TILE, TILE), f32)
            for n in range(negs):
                ds = ds + jnp.where(hits[n], weights[n : n + 1, :], 0.0)
            ds = ((ds - jnp.where(first, total, 0.0)) * inv_root).astype(bf16)
            dsc.append(ds)
            demb.append(dot(ds, cd, ((0,), (0,))))
        demb = jnp.concatenate(demb, axis=0)
        mean = jnp.mean(demb * embedding, axis=-1, keepdims=True)
        dhidden = scale * (demb - embedding * mean)
        dp = (dhidden * gate * (1.0 + preact * (1.0 - gate))).astype(bf16)
        dpre[at, :] = dp
        own[pl.ds(c * (step // BLK), step // BLK)] = dot(dp, top, ((1,), (1,))).reshape(
            step // BLK, BLK, width
        )
        dagg = (dot(dp, low, ((1,), (1,))) / degree).astype(bf16)
        for tt in range(CHUNK):
            t = c * CHUNK + tt
            cd, ct = tiles[tt]
            part = slice(tt * TILE, (tt + 1) * TILE)
            got = dot(dsc[tt], half[part, :], ((1,), (0,))) + dot(ct, dagg[part, :], ((1,), (0,)))
            dcand[pl.ds(t * NBT, NBT)] = got.reshape(NBT, BLK, width)
        return carry

    lax.fori_loop(0, rows // step, chunk, 0)

    wgrad[0:width, :] = dot(feat[...].reshape(rows, width), dpre[...], ((0,), (0,)))
    wgrad[width : 2 * width, :] = dot(agg[...], dpre[...], ((0,), (0,)))
    half_rows = width
    core = me & 1
    keep[0:half_rows, :] = wgrad[pl.ds(pl.multiple_of(core * half_rows, half_rows), half_rows), :]
    send[0:half_rows, :] = wgrad[
        pl.ds(pl.multiple_of((1 - core) * half_rows, half_rows), half_rows), :
    ]
    loss = jnp.sum(losses[...]) / negs
    spread = jnp.full((PAD, width), loss, f32)
    keep[half_rows : half_rows + PAD, :] = spread
    send[half_rows : half_rows + PAD, :] = spread

    def scatter(i, carry):
        d = where_own[i]
        to = jnp.maximum(d, 0)
        own[to] = own[to] + jnp.where(d >= 0, dcand[i], 0.0)
        return carry

    lax.fori_loop(0, blocks, scatter, 0, unroll=4)
    for k in range(1, peers):
        base = (me ^ k) * capacity

        def outgo(c, carry, k=k, base=base):
            back[k - 1][c] = dcand[where_slot[base + c]]
            return carry

        lax.fori_loop(0, capacity, outgo, 0, unroll=4)


def return_kernel(boundary, asked, own_in, *rest):
    grads, own = rest[:-1], rest[-1]
    own[...] = own_in[...]
    capacity = asked.shape[1]
    for k, got in enumerate(grads):

        def body(c, carry, k=k, got=got):
            to = boundary[asked[k, c]]
            own[to] = own[to] + got[c]
            return carry

        lax.fori_loop(0, capacity, body, 0, unroll=4)


def fold_kernel(masks, mine, other, keep, send):
    quarter = keep.shape[0] - PAD
    q = upper(masks, 0)
    for out, at in ((keep, q), (send, 1 - q)):
        rows = pl.ds(pl.multiple_of(at * quarter, quarter), quarter)
        out[0:quarter, :] = mine[rows, :] + other[rows, :]
        out[quarter:, :] = mine[2 * quarter :, :] + other[2 * quarter :, :]


def upper(masks, flip):
    i = lax.axis_index("dom") * lax.axis_size("group") + lax.axis_index("group")
    core = (i & 1) ^ flip
    return (i & jnp.where(core == 0, masks[0], masks[1]) != 0).astype(jnp.int32)


def finish_kernel(masks, rows, nodes, mine, far, theirs, theirs_far, wgrad, loss):
    quarter = mine.shape[0] - PAD
    core = lax.axis_index("group") & 1
    for flip, pair in ((0, (mine, far)), (1, (theirs, theirs_far))):
        q = upper(masks, flip)
        for at, got in zip((q, 1 - q), pair):
            to = ((core ^ flip) * 2 + at) * quarter
            wgrad[pl.ds(pl.multiple_of(to, quarter), quarter), :] = got[0:quarter, :] / rows
    first = jnp.where(core == 0, mine[quarter:, 0:128], theirs[quarter:, 0:128])
    loss[0, 0] = jnp.max(first) / nodes


def per_device(features, boundary, request, tile_slots, neighbors, negatives, layer_weight):
    row_count, width = features.shape
    peers = lax.axis_size("group")
    domains = lax.axis_size("dom")
    devices = peers * domains
    capacity = request.shape[1]
    bound_count = boundary.shape[0]
    block_count = row_count // BLK
    blocks = features.reshape(block_count, BLK, width)
    nbr = neighbors.T
    neg = negatives.T
    slots = tile_slots.T
    sds = jax.ShapeDtypeStruct

    shared = call(
        share_kernel,
        sds((bound_count + 1, BLK, width), bf16),
        (boundary, request, blocks),
        [SMEM, SMEM, VMEM],
        VMEM,
    )
    pieces = {0: shared}
    bit = peers // 2
    while bit:
        for k in list(pieces):
            pairs = [(i, i ^ bit) for i in range(peers)]
            pieces[k | bit] = lax.ppermute(pieces[k], "group", pairs)
        bit //= 2

    counts, pre, where_own, where_slot = call(
        early_kernel,
        (
            sds((row_count, TILE), bf16),
            sds((row_count, width), f32),
            sds((block_count,), jnp.int32),
            sds((peers * capacity + 1,), jnp.int32),
        ),
        (slots, request, boundary, features, layer_weight, nbr),
        [SMEM] * 3 + [VMEM] * 3,
        (VMEM, VMEM, SMEM, SMEM),
        flops=2 * row_count * width * width * 8,
    )
    outs = call(
        functools.partial(main_kernel, peers),
        (
            sds((block_count, BLK, width), f32),
            sds((width + PAD, width), f32),
            sds((width + PAD, width), f32),
        )
        + (sds((capacity, BLK, width), f32),) * (peers - 1),
        (request, where_own, where_slot, blocks, layer_weight, nbr, neg, pre, counts)
        + tuple(pieces[k] for k in range(1, peers)),
        [SMEM] * 3 + [VMEM] * (5 + peers),
        (VMEM,) * (peers + 2),
        scratch=(
            pltpu.VMEM((block_count, BLK, width), bf16),
            pltpu.VMEM((row_count, width), bf16),
            pltpu.VMEM((row_count, width), bf16),
            pltpu.VMEM((block_count, BLK, width), f32),
            pltpu.VMEM((2 * width, width), f32),
            pltpu.VMEM((8, TILE), f32),
        ),
        flops=2 * row_count * width * width * 20,
        limit=32,
    )
    own, keep, send = outs[:3]
    back = outs[3:]

    everyone = ("dom", "group")

    def swap(x, masks):
        return lax.ppermute(x, everyone, [(i, i ^ masks[i & 1]) for i in range(devices)])

    grads = [
        lax.ppermute(back[k - 1], "group", [(i, i ^ k) for i in range(peers)])
        for k in range(1, peers)
    ]
    bits = [1 << b for b in range(1, devices.bit_length() - 1)]
    masks = bits[-2:] + [bits[-3], bits[0]] + bits[1:-3]
    stages = []
    for s in range(0, len(masks), 2):
        pair = (masks[s], masks[min(s + 1, len(masks) - 1)])
        stages += [pair, pair[::-1]][: len(masks) - s]
    split = stages[0]
    quarter = sds((width // 2 + PAD, width), f32)
    total, send = call(
        functools.partial(fold_kernel, split),
        (quarter, quarter),
        (keep, swap(send, (1, 1))),
        [VMEM, VMEM],
        (VMEM, VMEM),
    )
    total = total + swap(send, split)
    for pair in stages[1:]:
        total = total + swap(total, pair)
    far = swap(total, split)
    theirs = swap(total, (1, 1))
    theirs_far = swap(far, (1, 1))
    weight_grad, loss = call(
        functools.partial(finish_kernel, split, row_count, row_count * devices),
        (sds((2 * width, width), f32), sds((1, 1), f32)),
        (total, far, theirs, theirs_far),
        [VMEM] * 4,
        (VMEM, SMEM),
    )

    me = lax.axis_index("group")
    asked = jnp.stack(
        [
            lax.dynamic_slice_in_dim(pieces[k][bound_count], me, 1)[0, :capacity]
            for k in range(1, peers)
        ]
    ).astype(jnp.int32)
    feature_grad = call(
        return_kernel,
        sds((block_count, BLK, width), f32),
        (boundary, asked, own) + tuple(grads),
        [SMEM, SMEM] + [VMEM] * peers,
        VMEM,
    )
    return feature_grad.reshape(row_count, width), weight_grad, loss.reshape(())


def solution(mesh):
    return jax.shard_map(
        per_device,
        mesh=mesh,
        in_specs=(
            P(("dom", "group"), None),
            P(("dom", "group")),
            P(("dom", "group"), None),
            P(("dom", "group"), None),
            P(("dom", "group"), None),
            P(("dom", "group"), None),
            P(),
        ),
        out_specs=(P(("dom", "group"), None), P(), P()),
        check_vma=False,
    )
```

```python
import functools

import jax
import jax.numpy as jnp
from jax import lax
from jax.experimental import pallas as pl
from jax.experimental.pallas import tpu as pltpu
from jax.sharding import PartitionSpec as P


TILE = 128
BLK = 16
NBT = 8
PAD = 8
CHUNK = 4


margin = 0.5
epsilon = 1e-06

VMEM = pl.BlockSpec(memory_space=pltpu.VMEM)
SMEM = pl.BlockSpec(memory_space=pltpu.SMEM)
f32 = jnp.float32
bf16 = jnp.bfloat16


def dot(left, right, dims):
    return lax.dot_general(left, right, (dims, ((), ())), preferred_element_type=f32)


def call(kernel, out_shape, args, specs, out_specs, scratch=(), flops=0, limit=8):
    size = sum(a.size * a.dtype.itemsize for a in args)
    return pl.pallas_call(
        kernel,
        out_shape=out_shape,
        in_specs=specs,
        out_specs=out_specs,
        scratch_shapes=list(scratch),
        cost_estimate=pl.CostEstimate(flops=flops, bytes_accessed=size, transcendentals=0),
        compiler_params=pltpu.CompilerParams(vmem_limit_bytes=limit << 20),
    )(*args)


def share_kernel(boundary, request, feat, out):
    count = boundary.shape[0]

    def body(i, carry):
        out[i] = feat[boundary[i]]
        return carry

    lax.fori_loop(0, count, body, 0, unroll=8)
    rows, cols = request.shape
    row_ids = lax.broadcasted_iota(jnp.int32, (BLK, 128), 0)
    lane_ids = lax.broadcasted_iota(jnp.int32, (BLK, 128), 1)
    tag = jnp.zeros((BLK, 128), f32)
    for r in range(rows):
        for c in range(cols):
            tag = jnp.where((row_ids == r) & (lane_ids == c), request[r, c].astype(f32), tag)
    out[count] = jnp.zeros((BLK, feat.shape[2]), bf16)
    out[count, :, 0:128] = tag.astype(bf16)


def early_kernel(slots, request, boundary, feat, weight, nbr, counts, pre, where_own, where_slot):
    rows, width = feat.shape
    blocks = where_own.shape[0]
    capacity = request.shape[1]
    me = lax.axis_index("group")

    def place(i, carry):
        t = i // NBT
        s = slots[i - t * NBT, t]
        local = s < blocks
        r = jnp.maximum(s - blocks, 0)
        e = r // capacity
        at = request[e, r - e * capacity]
        mine = local | (e == me)
        own_at = jnp.where(local, s, boundary[at])
        where_own[i] = jnp.where(mine, own_at, -1)
        spare = where_slot.shape[0] - 1
        where_slot[jnp.where(local, spare, r)] = i
        return carry

    lax.fori_loop(0, blocks, place, 0, unroll=4)
    degree = nbr.shape[0]
    cand_ids = lax.broadcasted_iota(jnp.int32, (TILE, TILE), 0)
    top = weight[0:width, :]

    def body(t, carry):
        at = pl.ds(pl.multiple_of(t * TILE, TILE), TILE)
        ids = nbr[:, at]
        total = jnp.zeros((TILE, TILE), f32)
        for j in range(degree):
            total = total + jnp.where(ids[j : j + 1, :] == cand_ids, 1.0, 0.0)
        counts[at, :] = total.astype(bf16)
        return carry

    lax.fori_loop(0, rows // TILE, body, 0)
    step = CHUNK * TILE

    def dense(c, carry):
        at = pl.ds(pl.multiple_of(c * step, step), step)
        pre[at, :] = dot(feat[at, :], top, ((1,), (0,)))
        return carry

    lax.fori_loop(0, rows // step, dense, 0)


def main_kernel(peers, request, where_own, where_slot, feat, weight, nbr, neg, pre, counts, *rest):
    pieces = rest[: peers - 1]
    keep, send, halves, dpre, dsc, cand, agg, wgrad, losses = rest[peers - 1 :]
    blocks, _, width = feat.shape
    rows = blocks * BLK
    capacity = request.shape[1]
    degree = nbr.shape[0]
    negs = neg.shape[0]
    me = lax.axis_index("group")

    def fetch(i, carry):
        cand[i] = feat[jnp.maximum(where_own[i], 0)]
        return carry

    lax.fori_loop(0, blocks, fetch, 0, unroll=8)
    for k in range(1, peers):
        peer = me ^ k

        def fetch_far(c, carry, k=k, peer=peer):
            cand[where_slot[peer * capacity + c]] = pieces[k - 1][request[peer, c]]
            return carry

        lax.fori_loop(0, capacity, fetch_far, 0, unroll=8)
    losses[...] = jnp.zeros(losses.shape, f32)
    low = weight[width : 2 * width, :]
    cand_ids = lax.broadcasted_iota(jnp.int32, (TILE, TILE), 0)
    step = CHUNK * TILE
    inv_root = width ** (-0.5)

    def chunk(c, carry):
        at = pl.ds(pl.multiple_of(c * step, step), step)
        tiles = []
        for tt in range(CHUNK):
            t = c * CHUNK + tt
            cd = cand[pl.ds(t * NBT, NBT)].reshape(TILE, width)
            ct = counts[pl.ds(pl.multiple_of(t * TILE, TILE), TILE), :]
            tiles.append((cd, ct))
            part = (dot(ct, cd, ((0,), (0,))) / degree).astype(bf16)
            agg[pl.ds(pl.multiple_of(t * TILE, TILE), TILE), :] = part
        preact = pre[at, :] + dot(agg[at, :], low, ((1,), (0,)))
        gate = jax.nn.sigmoid(preact)
        hidden = preact * gate
        scale = lax.rsqrt(jnp.mean(hidden * hidden, axis=-1, keepdims=True) + epsilon)
        embedding = hidden * scale
        half = embedding.astype(bf16)
        halves[at, :] = half
        demb = []
        for tt in range(CHUNK):
            t = c * CHUNK + tt
            lanes = pl.ds(pl.multiple_of(t * TILE, TILE), TILE)
            cd, ct = tiles[tt]
            scores = dot(cd, half[tt * TILE : (tt + 1) * TILE, :], ((1,), (1,))) * inv_root
            first = nbr[:, lanes][0:1, :] == cand_ids
            ids = neg[:, lanes]
            hits = [ids[n : n + 1, :] == cand_ids for n in range(negs)]
            pos = jnp.sum(jnp.where(first, scores, 0.0), axis=0, keepdims=True)
            picked = jnp.concatenate(
                [jnp.sum(jnp.where(h, scores, 0.0), axis=0, keepdims=True) for h in hits], axis=0
            )
            excess = margin + picked - pos
            soft = jnp.maximum(excess, 0.0) + jnp.log1p(jnp.exp(-jnp.abs(excess)))
            losses[0:negs, :] += soft
            weights = jax.nn.sigmoid(excess) / negs
            total = jnp.sum(weights, axis=0, keepdims=True)
            ds = jnp.zeros((TILE, TILE), f32)
            for n in range(negs):
                ds = ds + jnp.where(hits[n], weights[n : n + 1, :], 0.0)
            ds = ((ds - jnp.where(first, total, 0.0)) * inv_root).astype(bf16)
            dsc[lanes, :] = ds
            demb.append(dot(ds, cd, ((0,), (0,))))
        demb = jnp.concatenate(demb, axis=0)
        mean = jnp.mean(demb * embedding, axis=-1, keepdims=True)
        dhidden = scale * (demb - embedding * mean)
        dp = (dhidden * gate * (1.0 + preact * (1.0 - gate))).astype(bf16)
        dpre[at, :] = dp
        return carry

    lax.fori_loop(0, rows // step, chunk, 0)

    wgrad[0:width, :] = dot(feat[...].reshape(rows, width), dpre[...], ((0,), (0,)))
    wgrad[width : 2 * width, :] = dot(agg[...], dpre[...], ((0,), (0,)))
    half_rows = width
    core = me & 1
    keep[0:half_rows, :] = wgrad[pl.ds(pl.multiple_of(core * half_rows, half_rows), half_rows), :]
    send[0:half_rows, :] = wgrad[
        pl.ds(pl.multiple_of((1 - core) * half_rows, half_rows), half_rows), :
    ]
    loss = jnp.sum(losses[...]) / negs
    spread = jnp.full((PAD, width), loss, f32)
    keep[half_rows : half_rows + PAD, :] = spread
    send[half_rows : half_rows + PAD, :] = spread


def tail_kernel(degree, where_own, where_slot, weight, counts, halves, dpre, dsc, own, *rest):
    back, dcand = rest[:-1], rest[-1]
    rows, width = dpre.shape
    blocks = own.shape[0]
    capacity = back[0].shape[0]
    me = lax.axis_index("group")
    top = weight[0:width, :]
    low = weight[width : 2 * width, :]
    step = CHUNK * TILE

    def chunk(c, carry):
        at = pl.ds(pl.multiple_of(c * step, step), step)
        dp = dpre[at, :]
        own[pl.ds(c * (step // BLK), step // BLK)] = dot(dp, top, ((1,), (1,))).reshape(
            step // BLK, BLK, width
        )
        dagg = (dot(dp, low, ((1,), (1,))) / degree).astype(bf16)
        for tt in range(CHUNK):
            t = c * CHUNK + tt
            lanes = pl.ds(pl.multiple_of(t * TILE, TILE), TILE)
            part = slice(tt * TILE, (tt + 1) * TILE)
            got = dot(dsc[lanes, :], halves[lanes, :], ((1,), (0,)))
            got = got + dot(counts[lanes, :], dagg[part, :], ((1,), (0,)))
            dcand[pl.ds(t * NBT, NBT)] = got.reshape(NBT, BLK, width)
        return carry

    lax.fori_loop(0, rows // step, chunk, 0)

    def scatter(i, carry):
        d = where_own[i]
        to = jnp.maximum(d, 0)
        own[to] = own[to] + jnp.where(d >= 0, dcand[i], 0.0)
        return carry

    lax.fori_loop(0, blocks, scatter, 0, unroll=4)
    for k in range(1, len(back) + 1):
        base = (me ^ k) * capacity

        def outgo(c, carry, k=k, base=base):
            back[k - 1][c] = dcand[where_slot[base + c]]
            return carry

        lax.fori_loop(0, capacity, outgo, 0, unroll=4)


def return_kernel(boundary, asked, own_in, *rest):
    grads, own = rest[:-1], rest[-1]
    own[...] = own_in[...]
    capacity = asked.shape[1]
    for k, got in enumerate(grads):

        def body(c, carry, k=k, got=got):
            to = boundary[asked[k, c]]
            own[to] = own[to] + got[c]
            return carry

        lax.fori_loop(0, capacity, body, 0, unroll=4)


def fold_kernel(masks, mine, other, keep, send):
    quarter = keep.shape[0] - PAD
    q = upper(masks, 0)
    for out, at in ((keep, q), (send, 1 - q)):
        rows = pl.ds(pl.multiple_of(at * quarter, quarter), quarter)
        out[0:quarter, :] = mine[rows, :] + other[rows, :]
        out[quarter:, :] = mine[2 * quarter :, :] + other[2 * quarter :, :]


def upper(masks, flip):
    i = lax.axis_index("dom") * lax.axis_size("group") + lax.axis_index("group")
    core = (i & 1) ^ flip
    return (i & jnp.where(core == 0, masks[0], masks[1]) != 0).astype(jnp.int32)


def finish_kernel(masks, rows, nodes, mine, far, theirs, theirs_far, wgrad, loss):
    quarter = mine.shape[0] - PAD
    core = lax.axis_index("group") & 1
    for flip, pair in ((0, (mine, far)), (1, (theirs, theirs_far))):
        q = upper(masks, flip)
        for at, got in zip((q, 1 - q), pair):
            to = ((core ^ flip) * 2 + at) * quarter
            wgrad[pl.ds(pl.multiple_of(to, quarter), quarter), :] = got[0:quarter, :] / rows
    first = jnp.where(core == 0, mine[quarter:, 0:128], theirs[quarter:, 0:128])
    loss[0, 0] = jnp.max(first) / nodes


def per_device(features, boundary, request, tile_slots, neighbors, negatives, layer_weight):
    row_count, width = features.shape
    peers = lax.axis_size("group")
    domains = lax.axis_size("dom")
    devices = peers * domains
    capacity = request.shape[1]
    bound_count = boundary.shape[0]
    block_count = row_count // BLK
    blocks = features.reshape(block_count, BLK, width)
    nbr = neighbors.T
    neg = negatives.T
    slots = tile_slots.T
    sds = jax.ShapeDtypeStruct

    shared = call(
        share_kernel,
        sds((bound_count + 1, BLK, width), bf16),
        (boundary, request, blocks),
        [SMEM, SMEM, VMEM],
        VMEM,
        limit=60,
    )
    pieces = {0: shared}
    bit = peers // 2
    while bit:
        for k in list(pieces):
            pairs = [(i, i ^ bit) for i in range(peers)]
            pieces[k | bit] = lax.ppermute(pieces[k], "group", pairs)
        bit //= 2

    counts, pre, where_own, where_slot = call(
        early_kernel,
        (
            sds((row_count, TILE), bf16),
            sds((row_count, width), f32),
            sds((block_count,), jnp.int32),
            sds((peers * capacity + 1,), jnp.int32),
        ),
        (slots, request, boundary, features, layer_weight, nbr),
        [SMEM] * 3 + [VMEM] * 3,
        (VMEM, VMEM, SMEM, SMEM),
        flops=2 * row_count * width * width * 8,
    )
    wide = sds((row_count, width), bf16)
    part = sds((width + PAD, width), f32)
    keep, send, halves, dpre, dsc = call(
        functools.partial(main_kernel, peers),
        (part, part, wide, wide, sds((row_count, TILE), bf16)),
        (request, where_own, where_slot, blocks, layer_weight, nbr, neg, pre, counts)
        + tuple(pieces[k] for k in range(1, peers)),
        [SMEM] * 3 + [VMEM] * (5 + peers),
        (VMEM,) * 5,
        scratch=(
            pltpu.VMEM((block_count, BLK, width), bf16),
            pltpu.VMEM((row_count, width), bf16),
            pltpu.VMEM((2 * width, width), f32),
            pltpu.VMEM((8, TILE), f32),
        ),
        flops=2 * row_count * width * width * 16,
        limit=24,
    )
    own, *back = call(
        functools.partial(tail_kernel, nbr.shape[0]),
        (sds((block_count, BLK, width), f32),) + (sds((capacity, BLK, width), f32),) * (peers - 1),
        (where_own, where_slot, layer_weight, counts, halves, dpre, dsc),
        [SMEM] * 2 + [VMEM] * 5,
        (VMEM,) * peers,
        scratch=(pltpu.VMEM((block_count, BLK, width), f32),),
        flops=2 * row_count * width * width * 4,
        limit=16,
    )

    everyone = ("dom", "group")

    def swap(x, masks):
        return lax.ppermute(x, everyone, [(i, i ^ masks[i & 1]) for i in range(devices)])

    grads = [
        lax.ppermute(back[k - 1], "group", [(i, i ^ k) for i in range(peers)])
        for k in range(1, peers)
    ]
    bits = [1 << b for b in range(1, devices.bit_length() - 1)]
    masks = [bits[0], peers] + [b for b in bits[1:] if b != peers]
    stages = []
    for s in range(0, len(masks), 2):
        pair = (masks[s], masks[min(s + 1, len(masks) - 1)])
        stages += [pair, pair[::-1]][: len(masks) - s]
    split = stages[0]
    quarter = sds((width // 2 + PAD, width), f32)
    total, send = call(
        functools.partial(fold_kernel, split),
        (quarter, quarter),
        (keep, swap(send, (1, 1))),
        [VMEM, VMEM],
        (VMEM, VMEM),
    )
    total = total + swap(send, split)
    for pair in stages[1:]:
        total = total + swap(total, pair)
    far = swap(total, split)
    theirs = swap(total, (1, 1))
    theirs_far = swap(far, (1, 1))
    weight_grad, loss = call(
        functools.partial(finish_kernel, split, row_count, row_count * devices),
        (sds((2 * width, width), f32), sds((1, 1), f32)),
        (total, far, theirs, theirs_far),
        [VMEM] * 4,
        (VMEM, SMEM),
    )

    me = lax.axis_index("group")
    asked = jnp.stack(
        [
            lax.dynamic_slice_in_dim(pieces[k][bound_count], me, 1)[0, :capacity]
            for k in range(1, peers)
        ]
    ).astype(jnp.int32)
    feature_grad = call(
        return_kernel,
        sds((block_count, BLK, width), f32),
        (boundary, asked, own) + tuple(grads),
        [SMEM, SMEM] + [VMEM] * peers,
        VMEM,
    )
    return feature_grad.reshape(row_count, width), weight_grad, loss.reshape(())


def solution(mesh):
    return jax.shard_map(
        per_device,
        mesh=mesh,
        in_specs=(
            P(("dom", "group"), None),
            P(("dom", "group")),
            P(("dom", "group"), None),
            P(("dom", "group"), None),
            P(("dom", "group"), None),
            P(("dom", "group"), None),
            P(),
        ),
        out_specs=(P(("dom", "group"), None), P(), P()),
        check_vma=False,
    )
```

```python
import functools

import jax
import jax.numpy as jnp
from jax import lax
from jax.experimental import pallas as pl
from jax.experimental.pallas import tpu as pltpu
from jax.sharding import PartitionSpec as P


TILE = 128
BLK = 16
NBT = 8
PAD = 8
CHUNK = 4


margin = 0.5
epsilon = 1e-06

VMEM = pl.BlockSpec(memory_space=pltpu.VMEM)
SMEM = pl.BlockSpec(memory_space=pltpu.SMEM)
f32 = jnp.float32
bf16 = jnp.bfloat16


def dot(left, right, dims):
    return lax.dot_general(left, right, (dims, ((), ())), preferred_element_type=f32)


def call(kernel, out_shape, args, specs, out_specs, scratch=(), flops=0, limit=8):
    size = sum(a.size * a.dtype.itemsize for a in args)
    return pl.pallas_call(
        kernel,
        out_shape=out_shape,
        in_specs=specs,
        out_specs=out_specs,
        scratch_shapes=list(scratch),
        cost_estimate=pl.CostEstimate(flops=flops, bytes_accessed=size, transcendentals=0),
        compiler_params=pltpu.CompilerParams(vmem_limit_bytes=limit << 20),
    )(*args)


def share_kernel(boundary, request, feat, out):
    count = boundary.shape[0]

    def body(i, carry):
        out[i] = feat[boundary[i]]
        return carry

    lax.fori_loop(0, count, body, 0, unroll=8)
    rows, cols = request.shape
    row_ids = lax.broadcasted_iota(jnp.int32, (BLK, 128), 0)
    lane_ids = lax.broadcasted_iota(jnp.int32, (BLK, 128), 1)
    tag = jnp.zeros((BLK, 128), f32)
    for r in range(rows):
        for c in range(cols):
            tag = jnp.where((row_ids == r) & (lane_ids == c), request[r, c].astype(f32), tag)
    out[count] = jnp.zeros((BLK, feat.shape[2]), bf16)
    out[count, :, 0:128] = tag.astype(bf16)


def early_kernel(slots, request, boundary, feat, weight, nbr, counts, pre, where_own, where_slot):
    rows, width = feat.shape
    blocks = where_own.shape[0]
    capacity = request.shape[1]
    me = lax.axis_index("group")

    def place(i, carry):
        t = i // NBT
        s = slots[i - t * NBT, t]
        local = s < blocks
        r = jnp.maximum(s - blocks, 0)
        e = r // capacity
        at = request[e, r - e * capacity]
        mine = local | (e == me)
        own_at = jnp.where(local, s, boundary[at])
        where_own[i] = jnp.where(mine, own_at, -1)
        spare = where_slot.shape[0] - 1
        where_slot[jnp.where(local, spare, r)] = i
        return carry

    lax.fori_loop(0, blocks, place, 0, unroll=4)
    degree = nbr.shape[0]
    cand_ids = lax.broadcasted_iota(jnp.int32, (TILE, TILE), 0)
    top = weight[0:width, :]

    def body(t, carry):
        at = pl.ds(pl.multiple_of(t * TILE, TILE), TILE)
        ids = nbr[:, at]
        total = jnp.zeros((TILE, TILE), f32)
        for j in range(degree):
            total = total + jnp.where(ids[j : j + 1, :] == cand_ids, 1.0, 0.0)
        counts[at, :] = total.astype(bf16)
        return carry

    lax.fori_loop(0, rows // TILE, body, 0)
    step = CHUNK * TILE

    def dense(c, carry):
        at = pl.ds(pl.multiple_of(c * step, step), step)
        pre[at, :] = dot(feat[at, :], top, ((1,), (0,)))
        return carry

    lax.fori_loop(0, rows // step, dense, 0)


def main_kernel(peers, request, where_own, where_slot, feat, weight, nbr, neg, pre, counts, *rest):
    pieces = rest[: peers - 1]
    keep, send, halves, dpre, dsc, cand, agg, wgrad, losses = rest[peers - 1 :]
    blocks, _, width = feat.shape
    rows = blocks * BLK
    capacity = request.shape[1]
    degree = nbr.shape[0]
    negs = neg.shape[0]
    me = lax.axis_index("group")

    def fetch(i, carry):
        cand[i] = feat[jnp.maximum(where_own[i], 0)]
        return carry

    lax.fori_loop(0, blocks, fetch, 0, unroll=8)
    for k in range(1, peers):
        peer = me ^ k

        def fetch_far(c, carry, k=k, peer=peer):
            cand[where_slot[peer * capacity + c]] = pieces[k - 1][request[peer, c]]
            return carry

        lax.fori_loop(0, capacity, fetch_far, 0, unroll=8)
    losses[...] = jnp.zeros(losses.shape, f32)
    low = weight[width : 2 * width, :]
    cand_ids = lax.broadcasted_iota(jnp.int32, (TILE, TILE), 0)
    step = CHUNK * TILE
    inv_root = width ** (-0.5)

    def chunk(c, carry):
        at = pl.ds(pl.multiple_of(c * step, step), step)
        tiles = []
        for tt in range(CHUNK):
            t = c * CHUNK + tt
            cd = cand[pl.ds(t * NBT, NBT)].reshape(TILE, width)
            ct = counts[pl.ds(pl.multiple_of(t * TILE, TILE), TILE), :]
            tiles.append((cd, ct))
            part = (dot(ct, cd, ((0,), (0,))) / degree).astype(bf16)
            agg[pl.ds(pl.multiple_of(t * TILE, TILE), TILE), :] = part
        preact = pre[at, :] + dot(agg[at, :], low, ((1,), (0,)))
        gate = jax.nn.sigmoid(preact)
        hidden = preact * gate
        scale = lax.rsqrt(jnp.mean(hidden * hidden, axis=-1, keepdims=True) + epsilon)
        embedding = hidden * scale
        half = embedding.astype(bf16)
        halves[at, :] = half
        demb = []
        for tt in range(CHUNK):
            t = c * CHUNK + tt
            lanes = pl.ds(pl.multiple_of(t * TILE, TILE), TILE)
            cd, ct = tiles[tt]
            scores = dot(cd, half[tt * TILE : (tt + 1) * TILE, :], ((1,), (1,))) * inv_root
            first = nbr[:, lanes][0:1, :] == cand_ids
            ids = neg[:, lanes]
            hits = [ids[n : n + 1, :] == cand_ids for n in range(negs)]
            pos = jnp.sum(jnp.where(first, scores, 0.0), axis=0, keepdims=True)
            picked = jnp.concatenate(
                [jnp.sum(jnp.where(h, scores, 0.0), axis=0, keepdims=True) for h in hits], axis=0
            )
            excess = margin + picked - pos
            soft = jnp.maximum(excess, 0.0) + jnp.log1p(jnp.exp(-jnp.abs(excess)))
            losses[0:negs, :] += soft
            weights = jax.nn.sigmoid(excess) / negs
            total = jnp.sum(weights, axis=0, keepdims=True)
            ds = jnp.zeros((TILE, TILE), f32)
            for n in range(negs):
                ds = ds + jnp.where(hits[n], weights[n : n + 1, :], 0.0)
            ds = ((ds - jnp.where(first, total, 0.0)) * inv_root).astype(bf16)
            dsc[lanes, :] = ds
            demb.append(dot(ds, cd, ((0,), (0,))))
        demb = jnp.concatenate(demb, axis=0)
        mean = jnp.mean(demb * embedding, axis=-1, keepdims=True)
        dhidden = scale * (demb - embedding * mean)
        dp = (dhidden * gate * (1.0 + preact * (1.0 - gate))).astype(bf16)
        dpre[at, :] = dp
        return carry

    lax.fori_loop(0, rows // step, chunk, 0)

    wgrad[0:width, :] = dot(feat[...].reshape(rows, width), dpre[...], ((0,), (0,)))
    wgrad[width : 2 * width, :] = dot(agg[...], dpre[...], ((0,), (0,)))
    half_rows = width
    core = me & 1
    keep[0:half_rows, :] = wgrad[pl.ds(pl.multiple_of(core * half_rows, half_rows), half_rows), :]
    send[0:half_rows, :] = wgrad[
        pl.ds(pl.multiple_of((1 - core) * half_rows, half_rows), half_rows), :
    ]
    loss = jnp.sum(losses[...]) / negs
    spread = jnp.full((PAD, width), loss, f32)
    keep[half_rows : half_rows + PAD, :] = spread
    send[half_rows : half_rows + PAD, :] = spread


def agg_kernel(degree, weight, dpre, dagg):
    rows, width = dpre.shape
    low = weight[width : 2 * width, :]
    step = CHUNK * TILE

    def chunk(c, carry):
        at = pl.ds(pl.multiple_of(c * step, step), step)
        dagg[at, :] = (dot(dpre[at, :], low, ((1,), (1,))) / degree).astype(bf16)
        return carry

    lax.fori_loop(0, rows // step, chunk, 0)


def tail_kernel(where_own, where_slot, weight, counts, halves, dpre, dsc, dagg, own, *rest):
    back, dcand = rest[:-1], rest[-1]
    rows, width = dpre.shape
    blocks = own.shape[0]
    capacity = back[0].shape[0]
    me = lax.axis_index("group")
    top = weight[0:width, :]
    step = CHUNK * TILE

    def chunk(c, carry):
        at = pl.ds(pl.multiple_of(c * step, step), step)
        dp = dpre[at, :]
        own[pl.ds(c * (step // BLK), step // BLK)] = dot(dp, top, ((1,), (1,))).reshape(
            step // BLK, BLK, width
        )
        for tt in range(CHUNK):
            t = c * CHUNK + tt
            lanes = pl.ds(pl.multiple_of(t * TILE, TILE), TILE)
            got = dot(dsc[lanes, :], halves[lanes, :], ((1,), (0,)))
            got = got + dot(counts[lanes, :], dagg[lanes, :], ((1,), (0,)))
            dcand[pl.ds(t * NBT, NBT)] = got.reshape(NBT, BLK, width)
        return carry

    lax.fori_loop(0, rows // step, chunk, 0)

    def scatter(i, carry):
        d = where_own[i]
        to = jnp.maximum(d, 0)
        own[to] = own[to] + jnp.where(d >= 0, dcand[i], 0.0)
        return carry

    lax.fori_loop(0, blocks, scatter, 0, unroll=4)
    for k in range(1, len(back) + 1):
        base = (me ^ k) * capacity

        def outgo(c, carry, k=k, base=base):
            back[k - 1][c] = dcand[where_slot[base + c]]
            return carry

        lax.fori_loop(0, capacity, outgo, 0, unroll=4)


def return_kernel(boundary, asked, own_in, *rest):
    grads, own = rest[:-1], rest[-1]
    own[...] = own_in[...]
    capacity = asked.shape[1]
    for k, got in enumerate(grads):

        def body(c, carry, k=k, got=got):
            to = boundary[asked[k, c]]
            own[to] = own[to] + got[c]
            return carry

        lax.fori_loop(0, capacity, body, 0, unroll=4)


def fold_kernel(masks, mine, other, keep, send):
    quarter = keep.shape[0] - PAD
    q = upper(masks, 0)
    for out, at in ((keep, q), (send, 1 - q)):
        rows = pl.ds(pl.multiple_of(at * quarter, quarter), quarter)
        out[0:quarter, :] = mine[rows, :] + other[rows, :]
        out[quarter:, :] = mine[2 * quarter :, :] + other[2 * quarter :, :]


def upper(masks, flip):
    i = lax.axis_index("dom") * lax.axis_size("group") + lax.axis_index("group")
    core = (i & 1) ^ flip
    return (i & jnp.where(core == 0, masks[0], masks[1]) != 0).astype(jnp.int32)


def finish_kernel(masks, rows, nodes, mine, far, theirs, theirs_far, wgrad, loss):
    quarter = mine.shape[0] - PAD
    core = lax.axis_index("group") & 1
    for flip, pair in ((0, (mine, far)), (1, (theirs, theirs_far))):
        q = upper(masks, flip)
        for at, got in zip((q, 1 - q), pair):
            to = ((core ^ flip) * 2 + at) * quarter
            wgrad[pl.ds(pl.multiple_of(to, quarter), quarter), :] = got[0:quarter, :] / rows
    first = jnp.where(core == 0, mine[quarter:, 0:128], theirs[quarter:, 0:128])
    loss[0, 0] = jnp.max(first) / nodes


def per_device(features, boundary, request, tile_slots, neighbors, negatives, layer_weight):
    row_count, width = features.shape
    peers = lax.axis_size("group")
    domains = lax.axis_size("dom")
    devices = peers * domains
    capacity = request.shape[1]
    bound_count = boundary.shape[0]
    block_count = row_count // BLK
    blocks = features.reshape(block_count, BLK, width)
    nbr = neighbors.T
    neg = negatives.T
    slots = tile_slots.T
    sds = jax.ShapeDtypeStruct

    shared = call(
        share_kernel,
        sds((bound_count + 1, BLK, width), bf16),
        (boundary, request, blocks),
        [SMEM, SMEM, VMEM],
        VMEM,
        limit=60,
    )
    pieces = {0: shared}
    bit = peers // 2
    while bit:
        for k in list(pieces):
            pairs = [(i, i ^ bit) for i in range(peers)]
            pieces[k | bit] = lax.ppermute(pieces[k], "group", pairs)
        bit //= 2

    counts, pre, where_own, where_slot = call(
        early_kernel,
        (
            sds((row_count, TILE), bf16),
            sds((row_count, width), f32),
            sds((block_count,), jnp.int32),
            sds((peers * capacity + 1,), jnp.int32),
        ),
        (slots, request, boundary, features, layer_weight, nbr),
        [SMEM] * 3 + [VMEM] * 3,
        (VMEM, VMEM, SMEM, SMEM),
        flops=2 * row_count * width * width * 8,
    )
    wide = sds((row_count, width), bf16)
    part = sds((width + PAD, width), f32)
    keep, send, halves, dpre, dsc = call(
        functools.partial(main_kernel, peers),
        (part, part, wide, wide, sds((row_count, TILE), bf16)),
        (request, where_own, where_slot, blocks, layer_weight, nbr, neg, pre, counts)
        + tuple(pieces[k] for k in range(1, peers)),
        [SMEM] * 3 + [VMEM] * (5 + peers),
        (VMEM,) * 5,
        scratch=(
            pltpu.VMEM((block_count, BLK, width), bf16),
            pltpu.VMEM((row_count, width), bf16),
            pltpu.VMEM((2 * width, width), f32),
            pltpu.VMEM((8, TILE), f32),
        ),
        flops=2 * row_count * width * width * 16,
        limit=24,
    )
    dagg = call(
        functools.partial(agg_kernel, nbr.shape[0]),
        wide,
        (layer_weight, dpre),
        [VMEM] * 2,
        VMEM,
        flops=2 * row_count * width * width,
    )
    own, *back = call(
        tail_kernel,
        (sds((block_count, BLK, width), f32),) + (sds((capacity, BLK, width), f32),) * (peers - 1),
        (where_own, where_slot, layer_weight, counts, halves, dpre, dsc, dagg),
        [SMEM] * 2 + [VMEM] * 6,
        (VMEM,) * peers,
        scratch=(pltpu.VMEM((block_count, BLK, width), f32),),
        flops=2 * row_count * width * width * 4,
        limit=16,
    )

    everyone = ("dom", "group")

    def swap(x, masks):
        return lax.ppermute(x, everyone, [(i, i ^ masks[i & 1]) for i in range(devices)])

    grads = [
        lax.ppermute(back[k - 1], "group", [(i, i ^ k) for i in range(peers)])
        for k in range(1, peers)
    ]
    bits = [1 << b for b in range(1, devices.bit_length() - 1)]
    masks = [bits[0], peers] + [b for b in bits[1:] if b != peers]
    stages = []
    for s in range(0, len(masks), 2):
        pair = (masks[s], masks[min(s + 1, len(masks) - 1)])
        stages += [pair, pair[::-1]][: len(masks) - s]
    split = stages[0]
    quarter = sds((width // 2 + PAD, width), f32)
    total, send = call(
        functools.partial(fold_kernel, split),
        (quarter, quarter),
        (keep, swap(send, (1, 1))),
        [VMEM, VMEM],
        (VMEM, VMEM),
    )
    total = total + swap(send, split)
    for pair in stages[1:]:
        total = total + swap(total, pair)
    far = swap(total, split)
    theirs = swap(total, (1, 1))
    theirs_far = swap(total, (split[0] ^ 1, split[1] ^ 1))
    weight_grad, loss = call(
        functools.partial(finish_kernel, split, row_count, row_count * devices),
        (sds((2 * width, width), f32), sds((1, 1), f32)),
        (total, far, theirs, theirs_far),
        [VMEM] * 4,
        (VMEM, SMEM),
    )

    me = lax.axis_index("group")
    asked = jnp.stack(
        [
            lax.dynamic_slice_in_dim(pieces[k][bound_count], me, 1)[0, :capacity]
            for k in range(1, peers)
        ]
    ).astype(jnp.int32)
    feature_grad = call(
        return_kernel,
        sds((block_count, BLK, width), f32),
        (boundary, asked, own) + tuple(grads),
        [SMEM, SMEM] + [VMEM] * peers,
        VMEM,
    )
    return feature_grad.reshape(row_count, width), weight_grad, loss.reshape(())


def solution(mesh):
    return jax.shard_map(
        per_device,
        mesh=mesh,
        in_specs=(
            P(("dom", "group"), None),
            P(("dom", "group")),
            P(("dom", "group"), None),
            P(("dom", "group"), None),
            P(("dom", "group"), None),
            P(("dom", "group"), None),
            P(),
        ),
        out_specs=(P(("dom", "group"), None), P(), P()),
        check_vma=False,
    )
```
